32 devices in a mesh: elec: 4 (over y, core), pix: 8 (over z, x).
Axes of the slice: x: 2, y: 2, z: 4, core: 2. Of those that a mesh axis runs over, the one named last changes fastest.
Arguments:
- wavefronts: bfloat16 [1536, 2, 320, 256], P('elec', None, 'pix'), may hold values from -40 to 40, as said below
- trial_modes: float32 [2, 32, 320, 256], P(None, None, 'pix'), may hold values from -6 to 6
Outputs:
- sample_modes: float32 [2, 32, 320, 256], P(None, 'elec', None, 'pix')
The draws below stay inside these ranges and needn't reach their ends.
Inputs may be any that keep to these rules, and one draw needn't show every extreme that they name: `wavefronts`: field samples of each electron's wavefront.
All inputs are finite; a program needn't handle non-finite values.
Results may differ from the reference program's by a relative error of at most 0.0075.
Values may be sent and summed in bfloat16 or wider, within the bound.
A program may use at most 128 MiB of HBM per device.

```python
import math
import jax
import jax.numpy as jnp
from jax import lax

R = 320
C = 256
MODES = 32
ELEC_DEV = 384
ITERS = 2
NS_STEPS = 8
ELECTRONS = 1536
N_ELEC = 4


def draw_wavefronts(key, part):
    key_samples, key_rows, key_pixels = jax.random.split(key, 3)
    samples = jnp.clip(jax.random.normal(key_samples, (ELECTRONS, 2, R, C), jnp.float32), -4.0, 4.0)
    spread = math.log(10.0) / 2.0
    row_scale = jnp.exp(jax.random.uniform(key_rows, (ELECTRONS, 1, 1, 1), jnp.float32, 0.0, spread))
    pixel_scale = jnp.exp(jax.random.uniform(key_pixels, (1, 1, R, C), jnp.float32, 0.0, spread))
    return (samples * row_scale * pixel_scale).astype(jnp.bfloat16)


def shard_levels(rng, extent, cuts, low, top_value):
    loudness = 1.0
    for dim, shards_of in cuts:
        heights = jax.random.uniform(jax.random.fold_in(jax.random.fold_in(rng, 6), dim), (shards_of,), jnp.float32, low / len(cuts), top_value / len(cuts))
        loudness = loudness * jnp.repeat(jnp.exp(heights), extent[dim] // shards_of).reshape((-1,) + (1,) * (len(extent) - 1 - dim))
    return loudness


def scatter_about(key, extent, scale, bound, cuts=(), kind=jnp.bfloat16):
    loudness = shard_levels(key, extent, cuts, -0.22, 0.18) if cuts else 1.0
    array = jax.random.normal(key, extent, jnp.float32) * scale * loudness
    return jnp.minimum(jnp.maximum(array, -bound), bound).astype(kind)


def setup_inputs(seed: int = 0) -> dict:
    arg_keys = jax.random.split(jax.random.key(seed), 3)
    wavefronts = draw_wavefronts(jax.random.fold_in(arg_keys[2], 71), 0)
    trial_modes = scatter_about(arg_keys[1], (2, MODES, R, C), 1.0, 6.0, ((2, 8),), jnp.float32)
    return {"wavefronts": wavefronts, "trial_modes": trial_modes}


HIGH = lax.Precision.HIGHEST

def project(wave_re, wave_im, modes_low):
    stacked = modes_low.reshape(-1, modes_low.shape[2])
    swapped = jnp.concatenate([-modes_low[1], modes_low[0]], axis=0)
    contract = (((1,), (1,)), ((), ()))
    real_side = lax.dot_general(wave_re, stacked, contract, preferred_element_type=jnp.float32)
    imag_side = lax.dot_general(wave_im, swapped, contract, preferred_element_type=jnp.float32)
    return real_side + imag_side

def covariance(waves, projected, mode_count):
    pixels = waves.shape[1] // 2
    blocks = lax.dot_general(projected, waves.astype(jnp.float32), (((0,), (0,)), ((), ())), precision=HIGH, preferred_element_type=jnp.float32)
    real_part = blocks[:mode_count, :pixels] + blocks[mode_count:, pixels:]
    imag_part = blocks[mode_count:, :pixels] - blocks[:mode_count, pixels:]
    return jnp.stack([real_part, imag_part])

def gram_matrix(fields):
    flat = fields.reshape(-1, fields.shape[2])
    return jnp.dot(flat, flat.T, precision=HIGH)

def lowdin(gram_raw, mode_count):
    gram_re = gram_raw[:mode_count, :mode_count] + gram_raw[mode_count:, mode_count:]
    gram_im = gram_raw[:mode_count, mode_count:] - gram_raw[mode_count:, :mode_count]
    embedded = jnp.concatenate([jnp.concatenate([gram_re, -gram_im], 1), jnp.concatenate([gram_im, gram_re], 1)], 0)
    trace_value = jnp.trace(embedded)
    scaled = embedded / trace_value
    identity = jnp.eye(2 * mode_count, dtype=embedded.dtype)
    inverse_root = identity
    for iteration in range(NS_STEPS):
        correction = 1.5 * identity - 0.5 * jnp.dot(inverse_root, scaled, precision=HIGH)
        scaled = jnp.dot(scaled, correction, precision=HIGH)
        inverse_root = jnp.dot(correction, inverse_root, precision=HIGH)
    return (inverse_root / jnp.sqrt(trace_value)).T

def rotate(rotation, fields):
    flat = fields.reshape(-1, fields.shape[2])
    return jnp.dot(rotation, flat, precision=HIGH).reshape(fields.shape)

def dft_table(length):
    index = jnp.arange(length, dtype=jnp.int32)
    product = index[:, None] * index[None, :] % length
    angle = 2.0 * math.pi / length * product.astype(jnp.float32)
    return (jnp.cos(angle), -jnp.sin(angle))

def chirp_phase(row_pos, col_pos, row_total, col_total, factor):
    row_term = (row_pos - row_total / 2.0) ** 2 / row_total
    col_term = (col_pos - col_total / 2.0) ** 2 / col_total
    angle = math.pi * factor * (row_term[:, None] + col_term[None, :])
    return (jnp.cos(angle), jnp.sin(angle))

def column_section(field, row_pos, row_total, col_total):
    col_pos = jnp.arange(col_total, dtype=jnp.float32)
    chirp_re, chirp_im = chirp_phase(row_pos, col_pos, row_total, col_total, 0.5)
    launch_re = chirp_re * field[0] - chirp_im * field[1]
    launch_im = chirp_re * field[1] + chirp_im * field[0]
    table_re, table_im = dft_table(col_total)
    spec_re = jnp.einsum('mry,yv->mrv', launch_re, table_re, precision=HIGH) - jnp.einsum('mry,yv->mrv', launch_im, table_im, precision=HIGH)
    spec_im = jnp.einsum('mry,yv->mrv', launch_re, table_im, precision=HIGH) + jnp.einsum('mry,yv->mrv', launch_im, table_re, precision=HIGH)
    return jnp.stack([spec_re, spec_im])

def row_section(spectrum, col_pos, row_total, col_total):
    table_re, table_im = dft_table(row_total)
    out_re = jnp.einsum('ux,mxv->muv', table_re, spectrum[0], precision=HIGH) - jnp.einsum('ux,mxv->muv', table_im, spectrum[1], precision=HIGH)
    out_im = jnp.einsum('ux,mxv->muv', table_re, spectrum[1], precision=HIGH) + jnp.einsum('ux,mxv->muv', table_im, spectrum[0], precision=HIGH)
    row_pos = jnp.arange(row_total, dtype=jnp.float32)
    chirp_re, chirp_im = chirp_phase(row_pos, col_pos, row_total, col_total, 0.25)
    return jnp.stack([chirp_re * out_re - chirp_im * out_im, chirp_re * out_im + chirp_im * out_re])

def reference(wavefronts, trial_modes):
    pixels = R * C
    grouped = wavefronts.reshape(N_ELEC, ELEC_DEV, 2 * pixels)
    modes = trial_modes.reshape(2, MODES, pixels)
    for iteration in range(ITERS):
        modes_low = modes.astype(jnp.bfloat16)

        def group_sum(total, waves):
            projected = project(waves[:, :pixels], waves[:, pixels:], modes_low)
            return (total + covariance(waves, projected, MODES), None)
        applied, _ = lax.scan(group_sum, jnp.zeros((2, MODES, pixels), jnp.float32), grouped)
        modes = rotate(lowdin(gram_matrix(applied), MODES), applied)
    field = modes.reshape(2, MODES, R, C)
    spectrum = column_section(field, jnp.arange(R, dtype=jnp.float32), R, C)
    return row_section(spectrum, jnp.arange(C, dtype=jnp.float32), R, C)
```

```python
import functools
import math

import jax
import jax.numpy as jnp
import numpy as np
from jax import lax
from jax.experimental import pallas as pl
from jax.experimental.pallas import tpu as pltpu
from jax.sharding import PartitionSpec as P

ITERS = 2
NS_STEPS = 8

HIGH = lax.Precision.HIGHEST
MESH = pl.DeviceIdType.MESH


def greet(peers, axis):
    barrier = pltpu.get_barrier_semaphore()
    for peer in peers:
        pl.semaphore_signal(barrier, inc=1, device_id={axis: peer}, device_id_type=MESH)
    pl.semaphore_wait(barrier, len(peers))


def remote(src, dst, send_sem, recv_sem, axis, peer):
    return pltpu.make_async_remote_copy(
        src_ref=src,
        dst_ref=dst,
        send_sem=send_sem,
        recv_sem=recv_sem,
        device_id={axis: peer},
        device_id_type=MESH,
    )


def sum_kernel(n, axis, x_ref, out_ref, held, send_a, recv_a, send_b, recv_b):
    me = lax.axis_index(axis)
    peers = [lax.rem(me + d, n) for d in range(1, n)]
    greet(peers, axis)
    scatter = []
    for d in range(1, n):
        copy = remote(
            x_ref.at[peers[d - 1]], held.at[d], send_a.at[d], recv_a.at[d], axis, peers[d - 1]
        )
        copy.start()
        scatter.append(copy)
    total = x_ref[me]
    for d in range(1, n):
        scatter[d - 1].wait_recv()
        total = total + held[d]
    out_ref[me] = total
    gather = []
    for d in range(1, n):
        copy = remote(
            out_ref.at[me], out_ref.at[me], send_b.at[d], recv_b.at[d], axis, peers[d - 1]
        )
        copy.start()
        gather.append(copy)
    for d in range(1, n):
        source = lax.rem(me + n - d, n)
        remote(
            out_ref.at[source], out_ref.at[source], send_b.at[d], recv_b.at[d], axis, source
        ).wait_recv()
    for copy in scatter + gather:
        copy.wait_send()


def axis_sum(value, axis, collective_id):
    n = lax.axis_size(axis)
    rows, width = value.shape
    chunk = rows // n
    shape = (n, chunk, width)
    vmem = pl.BlockSpec(memory_space=pltpu.VMEM)
    dma = pltpu.SemaphoreType.DMA
    total = pl.pallas_call(
        functools.partial(sum_kernel, n, axis),
        out_shape=jax.ShapeDtypeStruct(shape, jnp.float32),
        in_specs=[vmem],
        out_specs=vmem,
        scratch_shapes=[pltpu.VMEM(shape, jnp.float32)] + [dma((n,))] * 4,
        compiler_params=pltpu.CompilerParams(collective_id=collective_id, has_side_effects=True),
        name=f"sum_{axis}_{collective_id}",
    )(value.reshape(shape))
    return total.reshape(rows, width)


def group_kernel(n, pieces, x_ref, out_ref, pair, half, far, sa, ra, sb, rb, sc, rc, sd, rd, se, re):
    me = lax.axis_index("elec")
    core = lax.rem(me, 2)
    chip = me // 2
    chips = n // 2
    partner = chip * 2 + 1 - core
    width = x_ref.shape[2] // pieces
    others = [lax.rem(chip + d, chips) for d in range(1, chips)]
    seats = [other * 2 + core for other in others]
    greet([partner] + seats, "elec")

    def part(ref, index, piece):
        return ref.at[index, :, pl.ds(piece * width, width)]

    def cut(piece):
        return pl.ds(piece * width, width)

    order = others + [chip]
    started = []
    first = {}
    for piece in range(pieces):
        for d, other in enumerate(order):
            slot = d * pieces + piece
            copy = remote(
                part(x_ref, other * 2 + 1 - core, piece),
                part(pair, d, piece),
                sa.at[slot],
                ra.at[slot],
                "elec",
                partner,
            )
            copy.start()
            started.append(copy)
            first[d, piece] = copy
    second = {}
    for piece in range(pieces):
        for d in range(chips - 1):
            slot = d * pieces + piece
            first[d, piece].wait_recv()
            half[d, :, cut(piece)] = (
                x_ref[seats[d], :, cut(piece)].astype(jnp.float32)
                + pair[d, :, cut(piece)].astype(jnp.float32)
            ).astype(jnp.bfloat16)
            copy = remote(
                part(half, d, piece), part(far, d, piece), sb.at[slot], rb.at[slot], "elec", seats[d]
            )
            copy.start()
            started.append(copy)
            second[d, piece] = copy
    for piece in range(pieces):
        first[chips - 1, piece].wait_recv()
        total = x_ref[me, :, cut(piece)].astype(jnp.float32) + pair[
            chips - 1, :, cut(piece)
        ].astype(jnp.float32)
        for d in range(chips - 1):
            second[d, piece].wait_recv()
            total = total + far[d, :, cut(piece)].astype(jnp.float32)
        out_ref[me, :, cut(piece)] = total.astype(jnp.bfloat16)
        for d in range(chips - 1):
            slot = d * pieces + piece
            copy = remote(
                part(out_ref, me, piece),
                part(out_ref, me, piece),
                sc.at[slot],
                rc.at[slot],
                "elec",
                seats[d],
            )
            copy.start()
            started.append(copy)
        copy = remote(
            part(out_ref, me, piece),
            part(out_ref, me, piece),
            sd.at[piece],
            rd.at[piece],
            "elec",
            partner,
        )
        copy.start()
        started.append(copy)
    for piece in range(pieces):
        for d in range(chips - 1):
            slot = d * pieces + piece
            source = lax.rem(chip + chips - 1 - d, chips) * 2 + core
            block = part(out_ref, source, piece)
            remote(block, block, sc.at[slot], rc.at[slot], "elec", source).wait_recv()
            copy = remote(block, block, se.at[slot], re.at[slot], "elec", partner)
            copy.start()
            started.append(copy)
    for piece in range(pieces):
        block = part(out_ref, partner, piece)
        remote(block, block, sd.at[piece], rd.at[piece], "elec", partner).wait_recv()
        for d in range(chips - 1):
            slot = d * pieces + piece
            source = lax.rem(chip + chips - 1 - d, chips) * 2 + 1 - core
            block = part(out_ref, source, piece)
            remote(block, block, se.at[slot], re.at[slot], "elec", partner).wait_recv()
    for copy in started:
        copy.wait_send()


def group_sum(value, collective_id):
    n = lax.axis_size("elec")
    rows, width = value.shape
    pieces = next(count for count in (4, 2, 1) if width % (128 * count) == 0)
    chips = n // 2
    chunk = rows // n
    shape = (n, chunk, width)
    vmem = pl.BlockSpec(memory_space=pltpu.VMEM)
    dma = pltpu.SemaphoreType.DMA
    slots = chips * pieces
    total = pl.pallas_call(
        functools.partial(group_kernel, n, pieces),
        out_shape=jax.ShapeDtypeStruct(shape, jnp.bfloat16),
        in_specs=[vmem],
        out_specs=vmem,
        scratch_shapes=[
            pltpu.VMEM((chips, chunk, width), jnp.bfloat16),
            pltpu.VMEM((chips, chunk, width), jnp.bfloat16),
            pltpu.VMEM((chips, chunk, width), jnp.bfloat16),
        ]
        + [dma((slots,))] * 10,
        compiler_params=pltpu.CompilerParams(collective_id=collective_id, has_side_effects=True),
        name=f"group_{collective_id}",
    )(value.reshape(shape))
    return total.reshape(rows, width)


def swap_kernel(n, axis, x_ref, out_ref, own_sem, send, recv):
    me = lax.axis_index(axis)
    peers = [lax.rem(me + d, n) for d in range(1, n)]
    greet(peers, axis)
    copies = []
    for d in range(1, n):
        copy = remote(
            x_ref.at[peers[d - 1]], out_ref.at[me], send.at[d], recv.at[d], axis, peers[d - 1]
        )
        copy.start()
        copies.append(copy)
    own = pltpu.make_async_copy(x_ref.at[me], out_ref.at[me], own_sem)
    own.start()
    own.wait()
    for d in range(1, n):
        source = lax.rem(me + n - d, n)
        remote(
            x_ref.at[source], out_ref.at[source], send.at[d], recv.at[d], axis, source
        ).wait_recv()
    for copy in copies:
        copy.wait_send()


def swap(value, axis, collective_id):
    n = lax.axis_size(axis)
    vmem = pl.BlockSpec(memory_space=pltpu.VMEM)
    dma = pltpu.SemaphoreType.DMA
    return pl.pallas_call(
        functools.partial(swap_kernel, n, axis),
        out_shape=jax.ShapeDtypeStruct(value.shape, value.dtype),
        in_specs=[vmem],
        out_specs=vmem,
        scratch_shapes=[dma, dma((n,)), dma((n,))],
        compiler_params=pltpu.CompilerParams(collective_id=collective_id, has_side_effects=True),
        name=f"swap_{axis}",
    )(value)


def project(wave_re, wave_im, stacked):
    half = stacked.shape[0] // 2
    swapped = jnp.concatenate([-stacked[half:], stacked[:half]], axis=0)
    contract = (((1,), (1,)), ((), ()))
    real_side = lax.dot_general(stacked, wave_re, contract, preferred_element_type=jnp.float32)
    imag_side = lax.dot_general(swapped, wave_im, contract, preferred_element_type=jnp.float32)
    return real_side + imag_side


def covariance(waves, projected, mode_count):
    pixels = waves.shape[1] // 2
    width = projected.shape[0]
    upper = lax.reduce_precision(projected, 8, 7)
    lower = (projected - upper).astype(jnp.bfloat16)
    both = jnp.concatenate([upper.astype(jnp.bfloat16), lower], axis=0)
    stacked = lax.dot_general(
        both, waves, (((1,), (0,)), ((), ())), preferred_element_type=jnp.float32
    )
    blocks = stacked[:width] + stacked[width:]
    real_part = blocks[:mode_count, :pixels] + blocks[mode_count:, pixels:]
    imag_part = blocks[mode_count:, :pixels] - blocks[:mode_count, pixels:]
    return jnp.concatenate([real_part, imag_part], axis=0)


def gram_matrix(flat):
    return lax.dot_general(flat, flat, (((1,), (1,)), ((), ())), preferred_element_type=jnp.float32)


def embed(gram_raw, mode_count):
    gram_re = gram_raw[:mode_count, :mode_count] + gram_raw[mode_count:, mode_count:]
    gram_im = gram_raw[:mode_count, mode_count:] - gram_raw[mode_count:, :mode_count]
    return jnp.concatenate(
        [jnp.concatenate([gram_re, -gram_im], 1), jnp.concatenate([gram_im, gram_re], 1)], 0
    )


def newton_schulz(scaled):
    identity = jnp.eye(scaled.shape[0], dtype=scaled.dtype)
    inverse_root = identity
    for step in range(NS_STEPS):
        product = scaled if step == 0 else jnp.dot(inverse_root, scaled, precision=HIGH)
        correction = 1.5 * identity - 0.5 * product
        if step == 0:
            inverse_root = correction
        else:
            inverse_root = jnp.dot(correction, inverse_root, precision=HIGH)
        if step + 1 < NS_STEPS:
            scaled = jnp.dot(scaled, correction, precision=HIGH)
    return inverse_root


def dft_table(length):
    index = np.arange(length, dtype=np.int64)
    angle = 2.0 * np.pi / length * (index[:, None] * index[None, :] % length)
    return np.cos(angle).astype(np.float32), -np.sin(angle).astype(np.float32)


def split(table):
    upper = table.astype(jnp.bfloat16)
    lower = (table - upper.astype(np.float32)).astype(jnp.bfloat16)
    return upper, lower


def chirp_phase(row_pos, col_pos, row_total, col_total, factor):
    row_term = (row_pos - row_total / 2.0) ** 2 / row_total
    col_term = (col_pos - col_total / 2.0) ** 2 / col_total
    angle = math.pi * factor * (row_term[:, None] + col_term[None, :])
    return (jnp.cos(angle), jnp.sin(angle))


def column_section(field, row_pos, row_total, col_total, pix_count):
    share, rows_dev = field.shape[1], field.shape[2]
    col_pos = jnp.arange(col_total, dtype=jnp.float32)
    chirp_re, chirp_im = chirp_phase(row_pos, col_pos, row_total, col_total, 0.5)
    launch_re = chirp_re * field[0] - chirp_im * field[1]
    launch_im = chirp_re * field[1] + chirp_im * field[0]
    table_re, table_im = dft_table(col_total)
    both = np.concatenate([table_re, table_im], axis=1)
    launch = jnp.stack([launch_re, launch_im]).reshape(2 * share * rows_dev, col_total)
    wide = jnp.dot(launch, jnp.asarray(both), precision=lax.Precision.HIGH)
    wide = wide.reshape(2, share, rows_dev, 2, pix_count, col_total // pix_count)
    spec_re = wide[0, :, :, 0] - wide[1, :, :, 1]
    spec_im = wide[0, :, :, 1] + wide[1, :, :, 0]
    spec = jnp.stack([spec_re, spec_im]).astype(jnp.bfloat16)
    return spec.transpose(3, 2, 0, 1, 4).reshape(pix_count, rows_dev, -1)


def row_section(spectrum, share, col_pos, row_total, col_total):
    width = col_pos.shape[0]
    table_re, table_im = dft_table(row_total)
    upper, lower = split(np.concatenate([table_re, table_im], axis=0))
    tables = np.concatenate([upper, lower], axis=0)
    wide = jnp.dot(jnp.asarray(tables), spectrum, preferred_element_type=jnp.float32)
    wide = wide[: 2 * row_total] + wide[2 * row_total :]
    half = share * width
    out_re = wide[:row_total, :half] - wide[row_total:, half:]
    out_im = wide[:row_total, half:] + wide[row_total:, :half]
    row_pos = jnp.arange(row_total, dtype=jnp.float32)
    chirp_re, chirp_im = chirp_phase(row_pos, col_pos, row_total, col_total, 0.25)
    out_re = out_re.reshape(row_total, share, width).transpose(1, 0, 2)
    out_im = out_im.reshape(row_total, share, width).transpose(1, 0, 2)
    return jnp.stack([chirp_re * out_re - chirp_im * out_im, chirp_re * out_im + chirp_im * out_re])


def shards(wavefronts, trial_modes):
    electrons_dev, _, rows_dev, cols = wavefronts.shape
    mode_count = trial_modes.shape[1]
    pixels = rows_dev * cols
    groups = lax.axis_size("elec")
    share = mode_count // groups
    waves = wavefronts.reshape(electrons_dev, 2 * pixels)
    wave_re = waves[:, :pixels]
    wave_im = waves[:, pixels:]
    low = trial_modes.astype(jnp.bfloat16).reshape(2 * mode_count, pixels)

    projected = axis_sum(project(wave_re, wave_im, low), "pix", 1)
    applied = group_sum(covariance(waves, projected, mode_count).astype(jnp.bfloat16), 2)

    turn = None
    for iteration in range(1, ITERS):
        gram_part = jnp.pad(gram_matrix(applied), ((0, 0), (0, -2 * mode_count % 128)))
        payload = jnp.concatenate([project(wave_re, wave_im, applied), gram_part], axis=1)
        summed = axis_sum(payload, "pix", 2 * iteration + 1)
        gram_raw = summed[:, electrons_dev : electrons_dev + 2 * mode_count]
        if turn is not None:
            gram_raw = jnp.dot(jnp.dot(turn, gram_raw, precision=HIGH), turn.T, precision=HIGH)
        embedded = embed(gram_raw, mode_count)
        trace_value = jnp.trace(embedded)
        step_turn = newton_schulz(embedded / trace_value).T
        turn = step_turn if turn is None else jnp.dot(step_turn, turn, precision=HIGH)
        projected = summed[:, :electrons_dev] * (1.0 / jnp.sqrt(trace_value))
        applied = group_sum(
            covariance(waves, projected, mode_count).astype(jnp.bfloat16), 2 * iteration + 2
        )
    gram_part = jnp.pad(gram_matrix(applied), ((0, 0), (0, -2 * mode_count % 128)))
    gram_raw = axis_sum(gram_part, "pix", 2 * ITERS + 1)[:, : 2 * mode_count]
    if turn is not None:
        gram_raw = jnp.dot(jnp.dot(turn, gram_raw, precision=HIGH), turn.T, precision=HIGH)
    embedded = embed(gram_raw, mode_count)
    trace_value = jnp.trace(embedded)
    last = (newton_schulz(embedded / trace_value) / jnp.sqrt(trace_value)).T
    turn = last if turn is None else jnp.dot(last, turn, precision=HIGH)
    mine = lax.dynamic_slice_in_dim(
        turn.reshape(2, mode_count, 2 * mode_count), lax.axis_index("elec") * share, share, axis=1
    ).reshape(2 * share, 2 * mode_count)
    mine_upper = lax.reduce_precision(mine, 8, 7)
    mine_lower = (mine - mine_upper).astype(jnp.bfloat16)
    field = jnp.dot(
        mine_upper.astype(jnp.bfloat16), applied, preferred_element_type=jnp.float32
    ) + jnp.dot(mine_lower, applied, preferred_element_type=jnp.float32)
    field = field.reshape(2, share, rows_dev, cols)

    pix_count = lax.axis_size("pix")
    row_total = rows_dev * pix_count
    row_pos = (lax.axis_index("pix") * rows_dev + jnp.arange(rows_dev, dtype=jnp.int32)).astype(
        jnp.float32
    )
    spectrum = column_section(field, row_pos, row_total, cols, pix_count)
    column_block = swap(spectrum, "pix", 2 * ITERS + 2).reshape(row_total, -1)
    width = cols // pix_count
    col_pos = (lax.axis_index("pix") * width + jnp.arange(width, dtype=jnp.int32)).astype(
        jnp.float32
    )
    return row_section(column_block, share, col_pos, row_total, cols)


def solution(mesh):
    in_specs = (P("elec", None, "pix", None), P(None, None, "pix", None))
    out_specs = P(None, "elec", None, "pix")
    return jax.shard_map(shards, mesh=mesh, in_specs=in_specs, out_specs=out_specs, check_vma=False)
```

```python
import functools
import math

import jax
import jax.numpy as jnp
import numpy as np
from jax import lax
from jax.experimental import pallas as pl
from jax.experimental.pallas import tpu as pltpu
from jax.sharding import PartitionSpec as P

NS_STEPS = 8

HIGH = lax.Precision.HIGHEST
MESH = pl.DeviceIdType.MESH


def greet(*groups):
    barrier = pltpu.get_barrier_semaphore()
    for axis, peers in groups:
        for peer in peers:
            pl.semaphore_signal(barrier, inc=1, device_id={axis: peer}, device_id_type=MESH)
    pl.semaphore_wait(barrier, sum(len(peers) for _, peers in groups))


def remote(src, dst, send_sem, recv_sem, axis, peer):
    return pltpu.make_async_remote_copy(
        src_ref=src,
        dst_ref=dst,
        send_sem=send_sem,
        recv_sem=recv_sem,
        device_id={axis: peer},
        device_id_type=MESH,
    )


NT = (((1,), (1,)), ((), ()))
NN = (((1,), (0,)), ((), ()))


def dot(left, right, dims):
    return lax.dot_general(left, right, dims, preferred_element_type=jnp.float32)


def scatter_gather(n, peers, x_ref, held, out_ref, send_a, recv_a, send_b, recv_b):
    me = lax.axis_index("pix")
    started = []
    scatter = []
    for d in range(1, n):
        peer = peers[d - 1]
        copy = remote(x_ref.at[peer], held.at[d], send_a.at[d], recv_a.at[d], "pix", peer)
        copy.start()
        scatter.append(copy)
    total = x_ref[me]
    for d in range(1, n):
        scatter[d - 1].wait_recv()
        total = total + held[d]
    out_ref[me] = total
    for d in range(1, n):
        copy = remote(
            out_ref.at[me], out_ref.at[me], send_b.at[d], recv_b.at[d], "pix", peers[d - 1]
        )
        copy.start()
        started.append(copy)
    for d in range(1, n):
        source = lax.rem(me + n - d, n)
        block = out_ref.at[source]
        remote(block, block, send_b.at[d], recv_b.at[d], "pix", source).wait_recv()
    return scatter + started


def core_kernel(
    np_, ne, pieces, sub, electrons, modes,
    waves_ref, part_ref,
    applied_ref, gram_ref, turn_ref,
    rows_a, both_ref, cut_ref, emb_ref,
    held_a, total_a, pay_ref, held_b, total_b,
    x_ref, pair, half, far, first_ref, gram_in,
    ps, es, gs,
):
    pixels = waves_ref.shape[1] // 2
    order = 2 * modes
    chunk = order // ne
    depth = order // np_
    width = pixels // pieces
    me_p = lax.axis_index("pix")
    peers = [lax.rem(me_p + d, np_) for d in range(1, np_)]
    me = lax.axis_index("elec")
    core = lax.rem(me, 2)
    chip = me // 2
    chips = ne // 2
    partner = chip * 2 + 1 - core
    others = [lax.rem(chip + d, chips) for d in range(1, chips)]
    seats = [other * 2 + core for other in others]
    sources = [lax.rem(chip + chips - d, chips) for d in range(1, chips)]
    greet(("pix", peers), ("elec", [partner] + seats))
    started = scatter_gather(
        np_, peers, part_ref, held_a, total_a, ps.at[0], ps.at[1], ps.at[2], ps.at[3]
    )
    for j in range(np_):
        rows_a[pl.ds(j * depth, depth), 0:electrons] = total_a[j]

    def split_rows(value):
        upper = value.astype(jnp.bfloat16)
        both_ref[0:order, :] = upper
        both_ref[order : 2 * order, :] = (value - upper.astype(jnp.float32)).astype(jnp.bfloat16)

    def part(ref, lead, piece):
        return ref.at[lead, :, pl.ds(piece * width, width)]

    def cut(piece):
        return pl.ds(piece * width, width)

    def round_trip(turn, gathered, finish, beside):
        sa, ra, sb, rb, sc, rc, sd, rd, se, re = [es.at[10 * turn + i] for i in range(10)]
        first, second = {}, {}

        def compute(piece):
            def body(step, carry):
                start = pl.multiple_of(piece * width + step * sub, 128)
                both = both_ref[...]
                from_re = dot(both, waves_ref[:, pl.ds(start, sub)], NN)
                from_im = dot(both, waves_ref[:, pl.ds(pl.multiple_of(pixels + start, 128), sub)], NN)
                from_re = from_re[:order] + from_re[order:]
                from_im = from_im[:order] + from_im[order:]
                real = from_re[:modes] + from_im[modes:]
                imag = from_re[modes:] - from_im[:modes]
                if chunk % 16 == 0:
                    whole = jnp.concatenate([real, imag], axis=0).astype(jnp.bfloat16)
                    for j in range(ne):
                        x_ref[turn, j, :, pl.ds(start, sub)] = whole[j * chunk : (j + 1) * chunk]
                else:
                    cut_ref[0:modes, :] = real
                    cut_ref[modes:order, :] = imag
                    for j in range(ne):
                        x_ref[turn, j, :, pl.ds(start, sub)] = cut_ref[
                            pl.ds(j * chunk, chunk), :
                        ].astype(jnp.bfloat16)
                return carry

            lax.fori_loop(0, width // sub, body, 0)
            for d, other in enumerate(others + [chip]):
                slot = d * pieces + piece
                copy = remote(
                    part(x_ref.at[turn], other * 2 + 1 - core, piece),
                    part(pair.at[turn], d, piece),
                    sa.at[slot], ra.at[slot], "elec", partner,
                )
                copy.start()
                started.append(copy)
                first[d, piece] = copy

        def cross(piece):
            for d in range(chips - 1):
                slot = d * pieces + piece
                first[d, piece].wait_recv()
                half[turn, d, :, cut(piece)] = (
                    x_ref[turn, seats[d], :, cut(piece)].astype(jnp.float32)
                    + pair[turn, d, :, cut(piece)].astype(jnp.float32)
                ).astype(jnp.bfloat16)
                copy = remote(
                    part(half.at[turn], d, piece), part(far.at[turn], d, piece),
                    sb.at[slot], rb.at[slot], "elec", seats[d],
                )
                copy.start()
                started.append(copy)
                second[d, piece] = copy

        def close(piece):
            first[chips - 1, piece].wait_recv()
            total = x_ref[turn, me, :, cut(piece)].astype(jnp.float32) + pair[
                turn, chips - 1, :, cut(piece)
            ].astype(jnp.float32)
            for d in range(chips - 1):
                second[d, piece].wait_recv()
                total = total + far[turn, d, :, cut(piece)].astype(jnp.float32)
            gathered[me, :, cut(piece)] = total.astype(jnp.bfloat16)
            block = part(gathered, me, piece)
            for d in range(chips - 1):
                slot = d * pieces + piece
                copy = remote(block, block, sc.at[slot], rc.at[slot], "elec", seats[d])
                copy.start()
                started.append(copy)
            copy = remote(block, block, sd.at[piece], rd.at[piece], "elec", partner)
            copy.start()
            started.append(copy)

        def relay(piece):
            for d in range(chips - 1):
                slot = d * pieces + piece
                source = sources[d] * 2 + core
                block = part(gathered, source, piece)
                remote(block, block, sc.at[slot], rc.at[slot], "elec", source).wait_recv()
                copy = remote(block, block, se.at[slot], re.at[slot], "elec", partner)
                copy.start()
                started.append(copy)

        def arrive(piece):
            block = part(gathered, partner, piece)
            remote(block, block, sd.at[piece], rd.at[piece], "elec", partner).wait_recv()
            for d in range(chips - 1):
                slot = d * pieces + piece
                block = part(gathered, sources[d] * 2 + 1 - core, piece)
                remote(block, block, se.at[slot], re.at[slot], "elec", partner).wait_recv()
            finish(piece)

        for tick in range(pieces + 5):
            for lag, stage in ((0, compute), (1, cross), (3, close), (4, relay), (5, arrive)):
                if 0 <= tick - lag < pieces:
                    stage(tick - lag)
            if tick == pieces:
                beside()

    def stacked(gathered, start):
        if chunk % 16 == 0:
            return jnp.concatenate([gathered[j, :, pl.ds(start, sub)] for j in range(ne)], axis=0)
        for j in range(ne):
            cut_ref[pl.ds(j * chunk, chunk), :] = gathered[j, :, pl.ds(start, sub)].astype(
                jnp.float32
            )
        return cut_ref[...].astype(jnp.bfloat16)

    wide = rows_a.shape[1]
    split_rows(rows_a[:, 0:electrons])
    rows_a[...] = jnp.zeros_like(rows_a)

    def project_piece(piece):
        def body(step, carry):
            start = pl.multiple_of(piece * width + step * sub, 128)
            fields = stacked(first_ref, start)
            swapped = jnp.concatenate([-fields[modes:], fields[:modes]], axis=0)
            rows_a[:, 0:electrons] += dot(fields, waves_ref[:, pl.ds(start, sub)], NT) + dot(
                swapped, waves_ref[:, pl.ds(pl.multiple_of(pixels + start, 128), sub)], NT
            )
            rows_a[:, electrons : electrons + order] += dot(fields, fields, NT)
            return carry

        lax.fori_loop(0, width // sub, body, 0)

    round_trip(0, first_ref, project_piece, lambda: None)
    for j in range(np_):
        pay_ref[j] = rows_a[pl.ds(j * depth, depth), :]
    started += scatter_gather(
        np_, peers, pay_ref, held_b, total_b, ps.at[4], ps.at[5], ps.at[6], ps.at[7]
    )
    for j in range(np_):
        rows_a[pl.ds(j * depth, depth), :] = total_b[j]

    row_id = lax.broadcasted_iota(jnp.int32, (order, order), 0)
    col_id = lax.broadcasted_iota(jnp.int32, (order, order), 1)
    raw = rows_a[:, electrons : electrons + order]
    trace = 2.0 * jnp.sum(
        jnp.sum(jnp.where(row_id == col_id, raw, 0.0), axis=1, keepdims=True), axis=0, keepdims=True
    )
    split_rows(rows_a[:, 0:electrons] / jnp.sqrt(trace))

    def first_turn():
        gram_re = raw[:modes, :modes] + raw[modes:, modes:]
        gram_im = raw[:modes, modes:] - raw[modes:, :modes]
        emb_ref[0:modes, 0:modes] = gram_re
        emb_ref[0:modes, modes:order] = -gram_im
        emb_ref[modes:order, 0:modes] = gram_im
        emb_ref[modes:order, modes:order] = gram_re
        identity = jnp.where(row_id == col_id, 1.0, 0.0).astype(jnp.float32)
        turn_ref[...] = newton_schulz(emb_ref[...] / trace, identity)

    emb2 = [jnp.zeros((order, order), jnp.float32)]

    def gram_piece(piece):
        def body(step, carry):
            fields = stacked(applied_ref, pl.multiple_of(piece * width + step * sub, 128))
            return carry + dot(fields, fields, NT)

        emb2[0] = lax.fori_loop(0, width // sub, body, emb2[0])

    round_trip(1, applied_ref, gram_piece, first_turn)
    raw2 = emb2[0]
    gram_re = raw2[:modes, :modes] + raw2[modes:, modes:]
    gram_im = raw2[:modes, modes:] - raw2[modes:, :modes]
    low = modes // 2
    emb_ref[0:modes, 0:modes] = gram_re
    emb_ref[0:modes, modes:order] = gram_im
    gram_in[0, :, 0:order] = emb_ref[0:low, 0:order]
    gram_in[0, :, order : 2 * order] = emb_ref[low:modes, 0:order]
    last = []
    for d in range(1, np_):
        copy = remote(
            gram_in.at[0], gram_in.at[d], gs.at[0, d], gs.at[1, d], "pix", peers[d - 1]
        )
        copy.start()
        last.append(copy)
    total = gram_in[0]
    for d in range(1, np_):
        last[d - 1].wait_recv()
        total = total + gram_in[d]
    gram_ref[...] = total
    for copy in started + last:
        copy.wait_send()


def middle(waves, part, mode_count):
    np_ = lax.axis_size("pix")
    ne = lax.axis_size("elec")
    electrons = waves.shape[0]
    pixels = waves.shape[1] // 2
    order = 2 * mode_count
    chunk = order // ne
    depth = order // np_
    pieces = next(count for count in (4, 2, 1) if pixels % (128 * count) == 0)
    sub = next(size for size in (512, 640, 256, 128) if pixels // pieces % size == 0)
    chips = ne // 2
    wide = electrons + order + -order % 128
    vmem = pl.BlockSpec(memory_space=pltpu.VMEM)
    dma = pltpu.SemaphoreType.DMA
    f32, bf16 = jnp.float32, jnp.bfloat16
    return pl.pallas_call(
        functools.partial(core_kernel, np_, ne, pieces, sub, electrons, mode_count),
        out_shape=[
            jax.ShapeDtypeStruct((ne, chunk, pixels), bf16),
            jax.ShapeDtypeStruct((mode_count // 2, 2 * order), f32),
            jax.ShapeDtypeStruct((order, order), f32),
        ],
        in_specs=[vmem, vmem],
        out_specs=[vmem] * 3,
        scratch_shapes=[
            pltpu.VMEM((order, wide), f32),
            pltpu.VMEM((2 * order, electrons), bf16),
            pltpu.VMEM((order, sub), f32),
            pltpu.VMEM((order, order), f32),
            pltpu.VMEM((np_, depth, electrons), f32),
            pltpu.VMEM((np_, depth, electrons), f32),
            pltpu.VMEM((np_, depth, wide), f32),
            pltpu.VMEM((np_, depth, wide), f32),
            pltpu.VMEM((np_, depth, wide), f32),
            pltpu.VMEM((2, ne, chunk, pixels), bf16),
            pltpu.VMEM((2, chips, chunk, pixels), bf16),
            pltpu.VMEM((2, chips, chunk, pixels), bf16),
            pltpu.VMEM((2, chips, chunk, pixels), bf16),
            pltpu.VMEM((ne, chunk, pixels), bf16),
            pltpu.VMEM((np_, mode_count // 2, 2 * order), f32),
            dma((8, np_)),
            dma((20, chips * pieces)),
            dma((2, np_)),
        ],
        compiler_params=pltpu.CompilerParams(
            collective_id=1, has_side_effects=True, vmem_limit_bytes=60 * 1024 * 1024
        ),
        name="middle",
    )(waves, part.reshape(np_, depth, electrons))


def swap_kernel(n, axis, x_ref, out_ref, own_sem, send, recv):
    me = lax.axis_index(axis)
    peers = [lax.rem(me + d, n) for d in range(1, n)]
    greet((axis, peers))
    copies = []
    for d in range(1, n):
        copy = remote(
            x_ref.at[peers[d - 1]], out_ref.at[me], send.at[d], recv.at[d], axis, peers[d - 1]
        )
        copy.start()
        copies.append(copy)
    own = pltpu.make_async_copy(x_ref.at[me], out_ref.at[me], own_sem)
    own.start()
    own.wait()
    for d in range(1, n):
        source = lax.rem(me + n - d, n)
        remote(
            x_ref.at[source], out_ref.at[source], send.at[d], recv.at[d], axis, source
        ).wait_recv()
    for copy in copies:
        copy.wait_send()


def swap(value, axis, collective_id):
    n = lax.axis_size(axis)
    vmem = pl.BlockSpec(memory_space=pltpu.VMEM)
    dma = pltpu.SemaphoreType.DMA
    return pl.pallas_call(
        functools.partial(swap_kernel, n, axis),
        out_shape=jax.ShapeDtypeStruct(value.shape, value.dtype),
        in_specs=[vmem],
        out_specs=vmem,
        scratch_shapes=[dma, dma((n,)), dma((n,))],
        compiler_params=pltpu.CompilerParams(collective_id=collective_id, has_side_effects=True),
        name=f"swap_{axis}",
    )(value)


def project(wave_re, wave_im, stacked):
    half = stacked.shape[0] // 2
    swapped = jnp.concatenate([-stacked[half:], stacked[:half]], axis=0)
    contract = (((1,), (1,)), ((), ()))
    real_side = lax.dot_general(stacked, wave_re, contract, preferred_element_type=jnp.float32)
    imag_side = lax.dot_general(swapped, wave_im, contract, preferred_element_type=jnp.float32)
    return real_side + imag_side


def embed(gram_raw, mode_count):
    gram_re = gram_raw[:mode_count, :mode_count] + gram_raw[mode_count:, mode_count:]
    gram_im = gram_raw[:mode_count, mode_count:] - gram_raw[mode_count:, :mode_count]
    return jnp.concatenate(
        [jnp.concatenate([gram_re, -gram_im], 1), jnp.concatenate([gram_im, gram_re], 1)], 0
    )


def newton_schulz(scaled, identity):
    inverse_root = identity
    for step in range(NS_STEPS):
        product = scaled if step == 0 else jnp.dot(inverse_root, scaled, precision=HIGH)
        correction = 1.5 * identity - 0.5 * product
        if step == 0:
            inverse_root = correction
        else:
            inverse_root = jnp.dot(correction, inverse_root, precision=HIGH)
        if step + 1 < NS_STEPS:
            scaled = jnp.dot(scaled, correction, precision=HIGH)
    return inverse_root


def dft_table(length):
    index = np.arange(length, dtype=np.int64)
    angle = 2.0 * np.pi / length * (index[:, None] * index[None, :] % length)
    return np.cos(angle).astype(np.float32), -np.sin(angle).astype(np.float32)


def split(table):
    upper = table.astype(jnp.bfloat16)
    lower = (table - upper.astype(np.float32)).astype(jnp.bfloat16)
    return upper, lower


def chirp_phase(row_pos, col_pos, row_total, col_total, factor):
    row_term = (row_pos - row_total / 2.0) ** 2 / row_total
    col_term = (col_pos - col_total / 2.0) ** 2 / col_total
    angle = math.pi * factor * (row_term[:, None] + col_term[None, :])
    return (jnp.cos(angle), jnp.sin(angle))


def column_section(field, row_pos, row_total, col_total, pix_count):
    share, rows_dev = field.shape[1], field.shape[2]
    col_pos = jnp.arange(col_total, dtype=jnp.float32)
    chirp_re, chirp_im = chirp_phase(row_pos, col_pos, row_total, col_total, 0.5)
    launch_re = chirp_re * field[0] - chirp_im * field[1]
    launch_im = chirp_re * field[1] + chirp_im * field[0]
    table_re, table_im = dft_table(col_total)
    both = np.concatenate([table_re, table_im], axis=1)
    launch = jnp.stack([launch_re, launch_im]).reshape(2 * share * rows_dev, col_total)
    wide = jnp.dot(launch, jnp.asarray(both), precision=lax.Precision.HIGH)
    wide = wide.reshape(2, share, rows_dev, 2, pix_count, col_total // pix_count)
    spec_re = wide[0, :, :, 0] - wide[1, :, :, 1]
    spec_im = wide[0, :, :, 1] + wide[1, :, :, 0]
    spec = jnp.stack([spec_re, spec_im]).astype(jnp.bfloat16)
    return spec.transpose(3, 2, 0, 1, 4).reshape(pix_count, rows_dev, -1)


def row_section(spectrum, share, col_pos, row_total, col_total):
    width = col_pos.shape[0]
    table_re, table_im = dft_table(row_total)
    upper, lower = split(np.concatenate([table_re, table_im], axis=0))
    tables = np.concatenate([upper, lower], axis=0)
    wide = jnp.dot(jnp.asarray(tables), spectrum, preferred_element_type=jnp.float32)
    wide = wide[: 2 * row_total] + wide[2 * row_total :]
    half = share * width
    out_re = wide[:row_total, :half] - wide[row_total:, half:]
    out_im = wide[:row_total, half:] + wide[row_total:, :half]
    row_pos = jnp.arange(row_total, dtype=jnp.float32)
    chirp_re, chirp_im = chirp_phase(row_pos, col_pos, row_total, col_total, 0.25)
    out_re = out_re.reshape(row_total, share, width).transpose(1, 0, 2)
    out_im = out_im.reshape(row_total, share, width).transpose(1, 0, 2)
    return jnp.stack([chirp_re * out_re - chirp_im * out_im, chirp_re * out_im + chirp_im * out_re])


def shards(wavefronts, trial_modes):
    electrons_dev, _, rows_dev, cols = wavefronts.shape
    mode_count = trial_modes.shape[1]
    order = 2 * mode_count
    pixels = rows_dev * cols
    groups = lax.axis_size("elec")
    share = mode_count // groups
    waves = wavefronts.reshape(electrons_dev, 2 * pixels)
    low = trial_modes.astype(jnp.bfloat16).reshape(order, pixels)

    part = project(waves[:, :pixels], waves[:, pixels:], low)
    applied, packed, inverse_root = middle(waves, part, mode_count)
    applied = applied.reshape(order, pixels)
    turn = inverse_root.T
    gram = jnp.concatenate([packed[:, :order], packed[:, order:]], axis=0)
    gram_re, gram_im = gram[:, :mode_count], gram[:, mode_count:]
    raw = jnp.concatenate(
        [jnp.concatenate([gram_re, gram_im], 1), jnp.concatenate([-gram_im, gram_re], 1)], 0
    )
    raw = 0.5 * jnp.dot(jnp.dot(turn, raw, precision=HIGH), inverse_root, precision=HIGH)
    embedded = embed(raw, mode_count)
    trace_value = jnp.trace(embedded)
    identity = jnp.eye(order, dtype=jnp.float32)
    last = (newton_schulz(embedded / trace_value, identity) / jnp.sqrt(trace_value)).T
    turn = jnp.dot(last, turn, precision=HIGH)
    mine = lax.dynamic_slice_in_dim(
        turn.reshape(2, mode_count, 2 * mode_count), lax.axis_index("elec") * share, share, axis=1
    ).reshape(2 * share, 2 * mode_count)
    mine_upper = lax.reduce_precision(mine, 8, 7)
    mine_lower = (mine - mine_upper).astype(jnp.bfloat16)
    field = jnp.dot(
        mine_upper.astype(jnp.bfloat16), applied, preferred_element_type=jnp.float32
    ) + jnp.dot(mine_lower, applied, preferred_element_type=jnp.float32)
    field = field.reshape(2, share, rows_dev, cols)

    pix_count = lax.axis_size("pix")
    row_total = rows_dev * pix_count
    row_pos = (lax.axis_index("pix") * rows_dev + jnp.arange(rows_dev, dtype=jnp.int32)).astype(
        jnp.float32
    )
    spectrum = column_section(field, row_pos, row_total, cols, pix_count)
    column_block = swap(spectrum, "pix", 2).reshape(row_total, -1)
    width = cols // pix_count
    col_pos = (lax.axis_index("pix") * width + jnp.arange(width, dtype=jnp.int32)).astype(
        jnp.float32
    )
    return row_section(column_block, share, col_pos, row_total, cols)


def solution(mesh):
    in_specs = (P("elec", None, "pix", None), P(None, None, "pix", None))
    out_specs = P(None, "elec", None, "pix")
    return jax.shard_map(shards, mesh=mesh, in_specs=in_specs, out_specs=out_specs, check_vma=False)
```

```python
import functools
import math

import jax
import jax.numpy as jnp
import numpy as np
from jax import lax
from jax.experimental import pallas as pl
from jax.experimental.pallas import tpu as pltpu
from jax.sharding import PartitionSpec as P

NS_STEPS = 8

HIGH = lax.Precision.HIGHEST
MESH = pl.DeviceIdType.MESH


def greet(*groups):
    barrier = pltpu.get_barrier_semaphore()
    for axis, peers in groups:
        for peer in peers:
            pl.semaphore_signal(barrier, inc=1, device_id={axis: peer}, device_id_type=MESH)
    pl.semaphore_wait(barrier, sum(len(peers) for _, peers in groups))


def remote(src, dst, send_sem, recv_sem, axis, peer):
    return pltpu.make_async_remote_copy(
        src_ref=src,
        dst_ref=dst,
        send_sem=send_sem,
        recv_sem=recv_sem,
        device_id={axis: peer},
        device_id_type=MESH,
    )


NT = (((1,), (1,)), ((), ()))
NN = (((1,), (0,)), ((), ()))


def dot(left, right, dims):
    return lax.dot_general(left, right, dims, preferred_element_type=jnp.float32)


def scatter_gather(n, peers, x_ref, held, out_ref, send_a, recv_a, send_b, recv_b):
    me = lax.axis_index("pix")
    started = []
    scatter = []
    for d in range(1, n):
        peer = peers[d - 1]
        copy = remote(x_ref.at[peer], held.at[d], send_a.at[d], recv_a.at[d], "pix", peer)
        copy.start()
        scatter.append(copy)
    total = x_ref[me]
    for d in range(1, n):
        scatter[d - 1].wait_recv()
        total = total + held[d]
    out_ref[me] = total
    for d in range(1, n):
        copy = remote(
            out_ref.at[me], out_ref.at[me], send_b.at[d], recv_b.at[d], "pix", peers[d - 1]
        )
        copy.start()
        started.append(copy)
    for d in range(1, n):
        source = lax.rem(me + n - d, n)
        block = out_ref.at[source]
        remote(block, block, send_b.at[d], recv_b.at[d], "pix", source).wait_recv()
    return scatter + started


def core_kernel(
    np_, ne, pieces, sub, electrons, modes,
    waves_ref, low_ref, chirp_ref, table_ref,
    out_ref,
    applied_ref, turn_ref, part_ref, lines_ref, launch_ref, spec_ref, send_ref, rows_a, both_ref, cut_ref, emb_ref,
    held_a, total_a, pay_ref, held_b, total_b,
    x_ref, pair, half, far, first_ref, gram_in,
    ps, es, gs,
):
    share = modes // ne
    rows, cols = chirp_ref.shape[1], chirp_ref.shape[2]
    pixels = waves_ref.shape[1] // 2
    order = 2 * modes
    chunk = order // ne
    depth = order // np_
    width = pixels // pieces
    me_p = lax.axis_index("pix")
    peers = [lax.rem(me_p + d, np_) for d in range(1, np_)]
    me = lax.axis_index("elec")
    core = lax.rem(me, 2)
    chip = me // 2
    chips = ne // 2
    partner = chip * 2 + 1 - core
    others = [lax.rem(chip + d, chips) for d in range(1, chips)]
    seats = [other * 2 + core for other in others]
    sources = [lax.rem(chip + chips - d, chips) for d in range(1, chips)]
    rows_a[...] = jnp.zeros_like(rows_a)

    def correlate(fields, start):
        swapped = jnp.concatenate([-fields[modes:], fields[:modes]], axis=0)
        rows_a[:, 0:electrons] += dot(fields, waves_ref[:, pl.ds(start, sub)], NT) + dot(
            swapped, waves_ref[:, pl.ds(pl.multiple_of(pixels + start, 128), sub)], NT
        )

    def opening(step, carry):
        start = pl.multiple_of(step * sub, 128)
        correlate(low_ref[:, pl.ds(start, sub)], start)
        return carry

    lax.fori_loop(0, pixels // sub, opening, 0)
    for j in range(np_):
        part_ref[j] = rows_a[pl.ds(j * depth, depth), 0:electrons]
    greet(("pix", peers), ("elec", [partner] + seats))
    started = scatter_gather(
        np_, peers, part_ref, held_a, total_a, ps.at[0], ps.at[1], ps.at[2], ps.at[3]
    )
    for j in range(np_):
        rows_a[pl.ds(j * depth, depth), 0:electrons] = total_a[j]

    def split_rows(value):
        upper = value.astype(jnp.bfloat16)
        both_ref[0:order, :] = upper
        both_ref[order : 2 * order, :] = (value - upper.astype(jnp.float32)).astype(jnp.bfloat16)

    def part(ref, lead, piece):
        return ref.at[lead, :, pl.ds(piece * width, width)]

    def cut(piece):
        return pl.ds(piece * width, width)

    def round_trip(turn, gathered, finish, beside):
        sa, ra, sb, rb, sc, rc, sd, rd, se, re = [es.at[10 * turn + i] for i in range(10)]
        first, second = {}, {}

        def compute(piece):
            def body(step, carry):
                start = pl.multiple_of(piece * width + step * sub, 128)
                both = both_ref[...]
                from_re = dot(both, waves_ref[:, pl.ds(start, sub)], NN)
                from_im = dot(both, waves_ref[:, pl.ds(pl.multiple_of(pixels + start, 128), sub)], NN)
                from_re = from_re[:order] + from_re[order:]
                from_im = from_im[:order] + from_im[order:]
                real = from_re[:modes] + from_im[modes:]
                imag = from_re[modes:] - from_im[:modes]
                if chunk % 16 == 0:
                    whole = jnp.concatenate([real, imag], axis=0).astype(jnp.bfloat16)
                    for j in range(ne):
                        x_ref[turn, j, :, pl.ds(start, sub)] = whole[j * chunk : (j + 1) * chunk]
                else:
                    cut_ref[0:modes, :] = real
                    cut_ref[modes:order, :] = imag
                    for j in range(ne):
                        x_ref[turn, j, :, pl.ds(start, sub)] = cut_ref[
                            pl.ds(j * chunk, chunk), :
                        ].astype(jnp.bfloat16)
                return carry

            lax.fori_loop(0, width // sub, body, 0)
            for d, other in enumerate(others + [chip]):
                slot = d * pieces + piece
                copy = remote(
                    part(x_ref.at[turn], other * 2 + 1 - core, piece),
                    part(pair.at[turn], d, piece),
                    sa.at[slot], ra.at[slot], "elec", partner,
                )
                copy.start()
                started.append(copy)
                first[d, piece] = copy

        def cross(piece):
            for d in range(chips - 1):
                slot = d * pieces + piece
                first[d, piece].wait_recv()
                half[turn, d, :, cut(piece)] = (
                    x_ref[turn, seats[d], :, cut(piece)].astype(jnp.float32)
                    + pair[turn, d, :, cut(piece)].astype(jnp.float32)
                ).astype(jnp.bfloat16)
                copy = remote(
                    part(half.at[turn], d, piece), part(far.at[turn], d, piece),
                    sb.at[slot], rb.at[slot], "elec", seats[d],
                )
                copy.start()
                started.append(copy)
                second[d, piece] = copy

        def close(piece):
            first[chips - 1, piece].wait_recv()
            total = x_ref[turn, me, :, cut(piece)].astype(jnp.float32) + pair[
                turn, chips - 1, :, cut(piece)
            ].astype(jnp.float32)
            for d in range(chips - 1):
                second[d, piece].wait_recv()
                total = total + far[turn, d, :, cut(piece)].astype(jnp.float32)
            gathered[me, :, cut(piece)] = total.astype(jnp.bfloat16)
            block = part(gathered, me, piece)
            for d in range(chips - 1):
                slot = d * pieces + piece
                copy = remote(block, block, sc.at[slot], rc.at[slot], "elec", seats[d])
                copy.start()
                started.append(copy)
            copy = remote(block, block, sd.at[piece], rd.at[piece], "elec", partner)
            copy.start()
            started.append(copy)

        def relay(piece):
            for d in range(chips - 1):
                slot = d * pieces + piece
                source = sources[d] * 2 + core
                block = part(gathered, source, piece)
                remote(block, block, sc.at[slot], rc.at[slot], "elec", source).wait_recv()
                copy = remote(block, block, se.at[slot], re.at[slot], "elec", partner)
                copy.start()
                started.append(copy)

        def arrive(piece):
            block = part(gathered, partner, piece)
            remote(block, block, sd.at[piece], rd.at[piece], "elec", partner).wait_recv()
            for d in range(chips - 1):
                slot = d * pieces + piece
                block = part(gathered, sources[d] * 2 + 1 - core, piece)
                remote(block, block, se.at[slot], re.at[slot], "elec", partner).wait_recv()
            finish(piece)

        for tick in range(pieces + 5):
            for lag, stage in ((0, compute), (1, cross), (3, close), (4, relay), (5, arrive)):
                if 0 <= tick - lag < pieces:
                    stage(tick - lag)
            if tick == pieces:
                beside()

    def stacked(gathered, start):
        if chunk % 16 == 0:
            return jnp.concatenate([gathered[j, :, pl.ds(start, sub)] for j in range(ne)], axis=0)
        for j in range(ne):
            cut_ref[pl.ds(j * chunk, chunk), :] = gathered[j, :, pl.ds(start, sub)].astype(
                jnp.float32
            )
        return cut_ref[...].astype(jnp.bfloat16)

    split_rows(rows_a[:, 0:electrons])
    rows_a[...] = jnp.zeros_like(rows_a)

    def project_piece(piece):
        def body(step, carry):
            start = pl.multiple_of(piece * width + step * sub, 128)
            fields = stacked(first_ref, start)
            correlate(fields, start)
            rows_a[:, electrons : electrons + order] += dot(fields, fields, NT)
            return carry

        lax.fori_loop(0, width // sub, body, 0)

    round_trip(0, first_ref, project_piece, lambda: None)
    for j in range(np_):
        pay_ref[j] = rows_a[pl.ds(j * depth, depth), :]
    started += scatter_gather(
        np_, peers, pay_ref, held_b, total_b, ps.at[4], ps.at[5], ps.at[6], ps.at[7]
    )
    for j in range(np_):
        rows_a[pl.ds(j * depth, depth), :] = total_b[j]

    row_id = lax.broadcasted_iota(jnp.int32, (order, order), 0)
    col_id = lax.broadcasted_iota(jnp.int32, (order, order), 1)
    raw = rows_a[:, electrons : electrons + order]
    trace = 2.0 * jnp.sum(
        jnp.sum(jnp.where(row_id == col_id, raw, 0.0), axis=1, keepdims=True), axis=0, keepdims=True
    )
    split_rows(rows_a[:, 0:electrons] / jnp.sqrt(trace))

    def first_turn():
        gram_re = raw[:modes, :modes] + raw[modes:, modes:]
        gram_im = raw[:modes, modes:] - raw[modes:, :modes]
        emb_ref[0:modes, 0:modes] = gram_re
        emb_ref[0:modes, modes:order] = -gram_im
        emb_ref[modes:order, 0:modes] = gram_im
        emb_ref[modes:order, modes:order] = gram_re
        identity = jnp.where(row_id == col_id, 1.0, 0.0).astype(jnp.float32)
        turn_ref[...] = newton_schulz(emb_ref[...] / trace, identity)

    emb2 = [jnp.zeros((order, order), jnp.float32)]

    def gram_piece(piece):
        def body(step, carry):
            fields = stacked(applied_ref, pl.multiple_of(piece * width + step * sub, 128))
            return carry + dot(fields, fields, NT)

        emb2[0] = lax.fori_loop(0, width // sub, body, emb2[0])

    round_trip(1, applied_ref, gram_piece, first_turn)
    raw2 = emb2[0]
    gram_re = raw2[:modes, :modes] + raw2[modes:, modes:]
    gram_im = raw2[:modes, modes:] - raw2[modes:, :modes]
    low = modes // 2
    emb_ref[0:modes, 0:modes] = gram_re
    emb_ref[0:modes, modes:order] = gram_im
    gram_in[0, :, 0:order] = emb_ref[0:low, 0:order]
    gram_in[0, :, order : 2 * order] = emb_ref[low:modes, 0:order]
    last = []
    for d in range(1, np_):
        copy = remote(
            gram_in.at[0], gram_in.at[d], gs.at[0, d], gs.at[1, d], "pix", peers[d - 1]
        )
        copy.start()
        last.append(copy)
    total = gram_in[0]
    for d in range(1, np_):
        last[d - 1].wait_recv()
        total = total + gram_in[d]
    emb_ref[0:low, 0:order] = total[:, 0:order]
    emb_ref[low:modes, 0:order] = total[:, order : 2 * order]
    gram_re = emb_ref[0:modes, 0:modes]
    gram_im = emb_ref[0:modes, modes:order]
    emb_ref[0:modes, modes:order] = gram_im
    emb_ref[modes:order, 0:modes] = -gram_im
    emb_ref[modes:order, modes:order] = gram_re
    first_root = turn_ref[...]
    first_t = first_root.T
    raw = 0.5 * jnp.dot(
        jnp.dot(first_t, emb_ref[...], precision=HIGH), first_root, precision=HIGH
    )
    gram_re = raw[:modes, :modes] + raw[modes:, modes:]
    gram_im = raw[:modes, modes:] - raw[modes:, :modes]
    emb_ref[0:modes, 0:modes] = gram_re
    emb_ref[0:modes, modes:order] = -gram_im
    emb_ref[modes:order, 0:modes] = gram_im
    emb_ref[modes:order, modes:order] = gram_re
    embedded = emb_ref[...]
    diagonal = row_id == col_id
    trace = jnp.sum(
        jnp.sum(jnp.where(diagonal, embedded, 0.0), axis=1, keepdims=True), axis=0, keepdims=True
    )
    identity = jnp.where(diagonal, 1.0, 0.0).astype(jnp.float32)
    second_root = newton_schulz(embedded / trace, identity) / jnp.sqrt(trace)
    turn_ref[...] = jnp.dot(second_root.T, first_t, precision=HIGH)
    for part_of in range(2):
        emb_ref[pl.ds(part_of * share, share), :] = turn_ref[
            pl.ds(part_of * modes + me * share, share), :
        ]
    mine = emb_ref[0 : 2 * share, :]
    upper = mine.astype(jnp.bfloat16)
    lower = (mine - upper.astype(jnp.float32)).astype(jnp.bfloat16)
    group = next(count for count in (8, 5, 4, 2, 1) if rows % count == 0)

    def rotate(step, carry):
        start = pl.multiple_of(step * (group * cols), 128)
        if chunk % 16 == 0:
            fields = jnp.concatenate(
                [applied_ref[j, :, pl.ds(start, group * cols)] for j in range(ne)], axis=0
            )
        else:
            fields = jnp.concatenate(
                [
                    applied_ref[j, :, pl.ds(start, group * cols)].astype(jnp.float32)
                    for j in range(ne)
                ],
                axis=0,
            ).astype(jnp.bfloat16)
        turned = dot(upper, fields, NN) + dot(lower, fields, NN)
        for i in range(group):
            for b in range(cols // 128):
                lines_ref[b, pl.ds((step * group + i) * 2 * share, 2 * share), :] = turned[
                    :, i * cols + b * 128 : i * cols + (b + 1) * 128
                ]
        return carry

    lax.fori_loop(0, rows // group, rotate, 0)
    chirp_re, chirp_im = chirp_ref[0], chirp_ref[1]
    for m in range(share):
        real = jnp.concatenate(
            [lines_ref[b, pl.ds(m, rows, stride=2 * share), :] for b in range(cols // 128)], axis=1
        )
        imag = jnp.concatenate(
            [
                lines_ref[b, pl.ds(share + m, rows, stride=2 * share), :]
                for b in range(cols // 128)
            ],
            axis=1,
        )
        launch_ref[m * rows : (m + 1) * rows, 0:cols] = chirp_re * real - chirp_im * imag
        launch_ref[m * rows : (m + 1) * rows, cols : 2 * cols] = chirp_re * imag + chirp_im * real
    launch = launch_ref[...]
    upper = launch.astype(jnp.bfloat16)
    lower = (launch - upper.astype(jnp.float32)).astype(jnp.bfloat16)
    spec_ref[...] = (
        dot(upper, table_ref[0], NN) + dot(upper, table_ref[1], NN) + dot(lower, table_ref[0], NN)
    )
    thin = cols // np_
    for p in range(np_):
        for c in range(2):
            for m in range(share):
                at = (2 * p + c) * thin
                to = (c * share + m) * thin
                send_ref[p, :, to : to + thin] = spec_ref[
                    m * rows : (m + 1) * rows, at : at + thin
                ].astype(jnp.bfloat16)
    swaps = []
    for d in range(1, np_):
        copy = remote(
            send_ref.at[peers[d - 1]], out_ref.at[me_p], gs.at[2, d], gs.at[3, d], "pix",
            peers[d - 1],
        )
        copy.start()
        swaps.append(copy)
    out_ref[me_p] = send_ref[me_p]
    for d in range(1, np_):
        source = lax.rem(me_p + np_ - d, np_)
        block = out_ref.at[source]
        remote(block, block, gs.at[2, d], gs.at[3, d], "pix", source).wait_recv()
    for copy in started + last + swaps:
        copy.wait_send()


def middle(waves, low, chirp, tables, mode_count):
    np_ = lax.axis_size("pix")
    ne = lax.axis_size("elec")
    electrons = waves.shape[0]
    pixels = waves.shape[1] // 2
    order = 2 * mode_count
    chunk = order // ne
    depth = order // np_
    pieces = next(count for count in (4, 2, 1) if pixels % (128 * count) == 0)
    sub = next(size for size in (512, 640, 256, 128) if pixels // pieces % size == 0)
    chips = ne // 2
    wide = electrons + order + -order % 128
    share = mode_count // ne
    rows, cols = chirp.shape[1:]
    lanes = 2 * share * (cols // np_)
    vmem = pl.BlockSpec(memory_space=pltpu.VMEM)
    dma = pltpu.SemaphoreType.DMA
    f32, bf16 = jnp.float32, jnp.bfloat16
    return pl.pallas_call(
        functools.partial(core_kernel, np_, ne, pieces, sub, electrons, mode_count),
        out_shape=jax.ShapeDtypeStruct((np_, rows, lanes), bf16),
        in_specs=[vmem] * 4,
        out_specs=vmem,
        scratch_shapes=[
            pltpu.VMEM((ne, chunk, pixels), bf16),
            pltpu.VMEM((order, order), f32),
            pltpu.VMEM((np_, depth, electrons), f32),
            pltpu.VMEM((cols // 128, rows * 2 * share, 128), f32),
            pltpu.VMEM((share * rows, 2 * cols), f32),
            pltpu.VMEM((share * rows, 2 * cols), f32),
            pltpu.VMEM((np_, rows, lanes), bf16),
            pltpu.VMEM((order, wide), f32),
            pltpu.VMEM((2 * order, electrons), bf16),
            pltpu.VMEM((order, sub), f32),
            pltpu.VMEM((order, order), f32),
            pltpu.VMEM((np_, depth, electrons), f32),
            pltpu.VMEM((np_, depth, electrons), f32),
            pltpu.VMEM((np_, depth, wide), f32),
            pltpu.VMEM((np_, depth, wide), f32),
            pltpu.VMEM((np_, depth, wide), f32),
            pltpu.VMEM((2, ne, chunk, pixels), bf16),
            pltpu.VMEM((2, chips, chunk, pixels), bf16),
            pltpu.VMEM((2, chips, chunk, pixels), bf16),
            pltpu.VMEM((2, chips, chunk, pixels), bf16),
            pltpu.VMEM((ne, chunk, pixels), bf16),
            pltpu.VMEM((np_, mode_count // 2, 2 * order), f32),
            dma((8, np_)),
            dma((20, chips * pieces)),
            dma((4, np_)),
        ],
        compiler_params=pltpu.CompilerParams(
            collective_id=1, has_side_effects=True, vmem_limit_bytes=60 * 1024 * 1024
        ),
        name="middle",
    )(waves, low, chirp, tables)


def newton_schulz(scaled, identity):
    inverse_root = identity
    for step in range(NS_STEPS):
        product = scaled if step == 0 else jnp.dot(inverse_root, scaled, precision=HIGH)
        correction = 1.5 * identity - 0.5 * product
        if step == 0:
            inverse_root = correction
        else:
            inverse_root = jnp.dot(correction, inverse_root, precision=HIGH)
        if step + 1 < NS_STEPS:
            scaled = jnp.dot(scaled, correction, precision=HIGH)
    return inverse_root


def dft_table(length):
    index = np.arange(length, dtype=np.int64)
    angle = 2.0 * np.pi / length * (index[:, None] * index[None, :] % length)
    return np.cos(angle).astype(np.float32), -np.sin(angle).astype(np.float32)


def split(table):
    upper = table.astype(jnp.bfloat16)
    lower = (table - upper.astype(np.float32)).astype(jnp.bfloat16)
    return upper, lower


def chirp_phase(row_pos, col_pos, row_total, col_total, factor):
    row_term = (row_pos - row_total / 2.0) ** 2 / row_total
    col_term = (col_pos - col_total / 2.0) ** 2 / col_total
    angle = math.pi * factor * (row_term[:, None] + col_term[None, :])
    return (jnp.cos(angle), jnp.sin(angle))


def column_tables(length, pix_count):
    table_re, table_im = dft_table(length)
    full = np.stack([np.stack([table_re, table_im], 1), np.stack([-table_im, table_re], 1)])
    full = full.reshape(2, length, 2, pix_count, length // pix_count).transpose(0, 1, 3, 2, 4)
    return np.stack(split(full.reshape(2 * length, 2 * length)))


def row_section(spectrum, share, col_pos, row_total, col_total):
    width = col_pos.shape[0]
    table_re, table_im = dft_table(row_total)
    upper, lower = split(np.concatenate([table_re, table_im], axis=0))
    tables = np.concatenate([upper, lower], axis=0)
    wide = jnp.dot(jnp.asarray(tables), spectrum, preferred_element_type=jnp.float32)
    wide = wide[: 2 * row_total] + wide[2 * row_total :]
    half = share * width
    out_re = wide[:row_total, :half] - wide[row_total:, half:]
    out_im = wide[:row_total, half:] + wide[row_total:, :half]
    row_pos = jnp.arange(row_total, dtype=jnp.float32)
    chirp_re, chirp_im = chirp_phase(row_pos, col_pos, row_total, col_total, 0.25)
    out_re = out_re.reshape(row_total, share, width).transpose(1, 0, 2)
    out_im = out_im.reshape(row_total, share, width).transpose(1, 0, 2)
    return jnp.stack([chirp_re * out_re - chirp_im * out_im, chirp_re * out_im + chirp_im * out_re])


def shards(wavefronts, trial_modes):
    electrons_dev, _, rows_dev, cols = wavefronts.shape
    mode_count = trial_modes.shape[1]
    order = 2 * mode_count
    pixels = rows_dev * cols
    groups = lax.axis_size("elec")
    share = mode_count // groups
    waves = wavefronts.reshape(electrons_dev, 2 * pixels)
    low = trial_modes.astype(jnp.bfloat16).reshape(order, pixels)

    pix_count = lax.axis_size("pix")
    row_total = rows_dev * pix_count
    row_pos = (lax.axis_index("pix") * rows_dev + jnp.arange(rows_dev, dtype=jnp.int32)).astype(
        jnp.float32
    )
    chirp = jnp.stack(
        chirp_phase(row_pos, jnp.arange(cols, dtype=jnp.float32), row_total, cols, 0.5)
    )
    tables = jnp.asarray(column_tables(cols, pix_count))
    column_block = middle(waves, low, chirp, tables, mode_count).reshape(row_total, -1)
    width = cols // pix_count
    col_pos = (lax.axis_index("pix") * width + jnp.arange(width, dtype=jnp.int32)).astype(
        jnp.float32
    )
    return row_section(column_block, share, col_pos, row_total, cols)


def solution(mesh):
    in_specs = (P("elec", None, "pix", None), P(None, None, "pix", None))
    out_specs = P(None, "elec", None, "pix")
    return jax.shard_map(shards, mesh=mesh, in_specs=in_specs, out_specs=out_specs, check_vma=False)
```

```python
import functools
import math

import jax
import jax.numpy as jnp
import numpy as np
from jax import lax
from jax.experimental import pallas as pl
from jax.experimental.pallas import tpu as pltpu
from jax.sharding import PartitionSpec as P

NS_STEPS = 8

HIGH = lax.Precision.HIGHEST
MESH = pl.DeviceIdType.MESH


def greet(*groups):
    barrier = pltpu.get_barrier_semaphore()
    for axis, peers in groups:
        for peer in peers:
            pl.semaphore_signal(barrier, inc=1, device_id={axis: peer}, device_id_type=MESH)
    return sum(len(peers) for _, peers in groups)


def remote(src, dst, send_sem, recv_sem, axis, peer):
    return pltpu.make_async_remote_copy(
        src_ref=src,
        dst_ref=dst,
        send_sem=send_sem,
        recv_sem=recv_sem,
        device_id={axis: peer},
        device_id_type=MESH,
    )


NT = (((1,), (1,)), ((), ()))
NN = (((1,), (0,)), ((), ()))


def dot(left, right, dims):
    return lax.dot_general(left, right, dims, preferred_element_type=jnp.float32)


def scatter_gather(n, peers, x_ref, held, out_ref, send_a, recv_a, send_b, recv_b):
    me = lax.axis_index("pix")
    started = []
    scatter = []
    for d in range(1, n):
        peer = peers[d - 1]
        copy = remote(x_ref.at[peer], held.at[d], send_a.at[d], recv_a.at[d], "pix", peer)
        copy.start()
        scatter.append(copy)
    total = x_ref[me]
    for d in range(1, n):
        scatter[d - 1].wait_recv()
        total = total + held[d]
    out_ref[me] = total
    for d in range(1, n):
        copy = remote(
            out_ref.at[me], out_ref.at[me], send_b.at[d], recv_b.at[d], "pix", peers[d - 1]
        )
        copy.start()
        started.append(copy)
    for d in range(1, n):
        source = lax.rem(me + n - d, n)
        block = out_ref.at[source]
        remote(block, block, send_b.at[d], recv_b.at[d], "pix", source).wait_recv()
    return scatter + started


def core_kernel(
    np_, ne, pieces, sub, electrons, modes,
    waves_ref, low_ref, chirp_ref, table_ref,
    out_ref,
    applied_ref, turn_ref, part_ref, lines_ref, launch_ref, spec_ref, send_ref, rows_a, both_ref, cut_ref, emb_ref,
    held_a, total_a, pay_ref, held_b, total_b,
    x_ref, pair, half, far, first_ref, gram_in,
    ps, es, gs,
):
    share = modes // ne
    rows, cols = chirp_ref.shape[1], chirp_ref.shape[2]
    pixels = waves_ref.shape[1] // 2
    order = 2 * modes
    chunk = order // ne
    depth = order // np_
    width = pixels // pieces
    me_p = lax.axis_index("pix")
    peers = [lax.rem(me_p + d, np_) for d in range(1, np_)]
    me = lax.axis_index("elec")
    core = lax.rem(me, 2)
    chip = me // 2
    chips = ne // 2
    partner = chip * 2 + 1 - core
    others = [lax.rem(chip + d, chips) for d in range(1, chips)]
    seats = [other * 2 + core for other in others]
    sources = [lax.rem(chip + chips - d, chips) for d in range(1, chips)]
    greeted = greet(("pix", peers), ("elec", [partner] + seats))
    rows_a[...] = jnp.zeros_like(rows_a)

    def correlate(fields, start):
        swapped = jnp.concatenate([-fields[modes:], fields[:modes]], axis=0)
        rows_a[:, 0:electrons] += dot(fields, waves_ref[:, pl.ds(start, sub)], NT) + dot(
            swapped, waves_ref[:, pl.ds(pl.multiple_of(pixels + start, 128), sub)], NT
        )

    def opening(step, carry):
        start = pl.multiple_of(step * sub, 128)
        correlate(low_ref[:, pl.ds(start, sub)], start)
        return carry

    lax.fori_loop(0, pixels // sub, opening, 0)
    for j in range(np_):
        part_ref[j] = rows_a[pl.ds(j * depth, depth), 0:electrons]
    pl.semaphore_wait(pltpu.get_barrier_semaphore(), greeted)
    started = scatter_gather(
        np_, peers, part_ref, held_a, total_a, ps.at[0], ps.at[1], ps.at[2], ps.at[3]
    )
    for j in range(np_):
        rows_a[pl.ds(j * depth, depth), 0:electrons] = total_a[j]

    def split_rows(value):
        upper = value.astype(jnp.bfloat16)
        both_ref[0:order, :] = upper
        both_ref[order : 2 * order, :] = (value - upper.astype(jnp.float32)).astype(jnp.bfloat16)

    def part(ref, lead, piece):
        return ref.at[lead, :, pl.ds(piece * width, width)]

    def cut(piece):
        return pl.ds(piece * width, width)

    def round_trip(turn, gathered, finish, beside):
        sa, ra, sb, rb, sc, rc, sd, rd, se, re = [es.at[10 * turn + i] for i in range(10)]
        first, second = {}, {}

        def compute(piece):
            def body(step, carry):
                start = pl.multiple_of(piece * width + step * sub, 128)
                both = both_ref[...]
                from_re = dot(both, waves_ref[:, pl.ds(start, sub)], NN)
                from_im = dot(both, waves_ref[:, pl.ds(pl.multiple_of(pixels + start, 128), sub)], NN)
                from_re = from_re[:order] + from_re[order:]
                from_im = from_im[:order] + from_im[order:]
                real = from_re[:modes] + from_im[modes:]
                imag = from_re[modes:] - from_im[:modes]
                if chunk % 16 == 0:
                    whole = jnp.concatenate([real, imag], axis=0).astype(jnp.bfloat16)
                    for j in range(ne):
                        x_ref[turn, j, :, pl.ds(start, sub)] = whole[j * chunk : (j + 1) * chunk]
                else:
                    cut_ref[0:modes, :] = real
                    cut_ref[modes:order, :] = imag
                    for j in range(ne):
                        x_ref[turn, j, :, pl.ds(start, sub)] = cut_ref[
                            pl.ds(j * chunk, chunk), :
                        ].astype(jnp.bfloat16)
                return carry

            lax.fori_loop(0, width // sub, body, 0)
            for d, other in enumerate(others + [chip]):
                slot = d * pieces + piece
                copy = remote(
                    part(x_ref.at[turn], other * 2 + 1 - core, piece),
                    part(pair.at[turn], d, piece),
                    sa.at[slot], ra.at[slot], "elec", partner,
                )
                copy.start()
                started.append(copy)
                first[d, piece] = copy

        def cross(piece):
            for d in range(chips - 1):
                slot = d * pieces + piece
                first[d, piece].wait_recv()
                half[turn, d, :, cut(piece)] = (
                    x_ref[turn, seats[d], :, cut(piece)].astype(jnp.float32)
                    + pair[turn, d, :, cut(piece)].astype(jnp.float32)
                ).astype(jnp.bfloat16)
                copy = remote(
                    part(half.at[turn], d, piece), part(far.at[turn], d, piece),
                    sb.at[slot], rb.at[slot], "elec", seats[d],
                )
                copy.start()
                started.append(copy)
                second[d, piece] = copy

        def close(piece):
            first[chips - 1, piece].wait_recv()
            total = x_ref[turn, me, :, cut(piece)].astype(jnp.float32) + pair[
                turn, chips - 1, :, cut(piece)
            ].astype(jnp.float32)
            for d in range(chips - 1):
                second[d, piece].wait_recv()
                total = total + far[turn, d, :, cut(piece)].astype(jnp.float32)
            gathered[me, :, cut(piece)] = total.astype(jnp.bfloat16)
            block = part(gathered, me, piece)
            for d in range(chips - 1):
                slot = d * pieces + piece
                copy = remote(block, block, sc.at[slot], rc.at[slot], "elec", seats[d])
                copy.start()
                started.append(copy)
            copy = remote(block, block, sd.at[piece], rd.at[piece], "elec", partner)
            copy.start()
            started.append(copy)

        def relay(piece):
            for d in range(chips - 1):
                slot = d * pieces + piece
                source = sources[d] * 2 + core
                block = part(gathered, source, piece)
                remote(block, block, sc.at[slot], rc.at[slot], "elec", source).wait_recv()
                copy = remote(block, block, se.at[slot], re.at[slot], "elec", partner)
                copy.start()
                started.append(copy)

        def arrive(piece):
            block = part(gathered, partner, piece)
            remote(block, block, sd.at[piece], rd.at[piece], "elec", partner).wait_recv()
            for d in range(chips - 1):
                slot = d * pieces + piece
                block = part(gathered, sources[d] * 2 + 1 - core, piece)
                remote(block, block, se.at[slot], re.at[slot], "elec", partner).wait_recv()
            finish(piece)

        for tick in range(pieces + 5):
            for lag, stage in ((0, compute), (1, cross), (3, close), (4, relay), (5, arrive)):
                if 0 <= tick - lag < pieces:
                    stage(tick - lag)
            if tick == pieces:
                beside()

    def stacked(gathered, start):
        if chunk % 16 == 0:
            return jnp.concatenate([gathered[j, :, pl.ds(start, sub)] for j in range(ne)], axis=0)
        for j in range(ne):
            cut_ref[pl.ds(j * chunk, chunk), :] = gathered[j, :, pl.ds(start, sub)].astype(
                jnp.float32
            )
        return cut_ref[...].astype(jnp.bfloat16)

    split_rows(rows_a[:, 0:electrons])
    rows_a[...] = jnp.zeros_like(rows_a)

    def project_piece(piece):
        def body(step, carry):
            start = pl.multiple_of(piece * width + step * sub, 128)
            fields = stacked(first_ref, start)
            correlate(fields, start)
            rows_a[:, electrons : electrons + order] += dot(fields, fields, NT)
            return carry

        lax.fori_loop(0, width // sub, body, 0)

    round_trip(0, first_ref, project_piece, lambda: None)
    for j in range(np_):
        pay_ref[j] = rows_a[pl.ds(j * depth, depth), :]
    started += scatter_gather(
        np_, peers, pay_ref, held_b, total_b, ps.at[4], ps.at[5], ps.at[6], ps.at[7]
    )
    for j in range(np_):
        rows_a[pl.ds(j * depth, depth), :] = total_b[j]

    row_id = lax.broadcasted_iota(jnp.int32, (order, order), 0)
    col_id = lax.broadcasted_iota(jnp.int32, (order, order), 1)
    raw = rows_a[:, electrons : electrons + order]
    trace = 2.0 * jnp.sum(
        jnp.sum(jnp.where(row_id == col_id, raw, 0.0), axis=1, keepdims=True), axis=0, keepdims=True
    )
    split_rows(rows_a[:, 0:electrons] / jnp.sqrt(trace))

    def first_turn():
        gram_re = raw[:modes, :modes] + raw[modes:, modes:]
        gram_im = raw[:modes, modes:] - raw[modes:, :modes]
        emb_ref[0:modes, 0:modes] = gram_re
        emb_ref[0:modes, modes:order] = -gram_im
        emb_ref[modes:order, 0:modes] = gram_im
        emb_ref[modes:order, modes:order] = gram_re
        identity = jnp.where(row_id == col_id, 1.0, 0.0).astype(jnp.float32)
        turn_ref[...] = newton_schulz(emb_ref[...] / trace, identity)

    emb2 = [jnp.zeros((order, order), jnp.float32)]

    def gram_piece(piece):
        def body(step, carry):
            fields = stacked(applied_ref, pl.multiple_of(piece * width + step * sub, 128))
            return carry + dot(fields, fields, NT)

        emb2[0] = lax.fori_loop(0, width // sub, body, emb2[0])

    round_trip(1, applied_ref, gram_piece, first_turn)
    raw2 = emb2[0]
    gram_re = raw2[:modes, :modes] + raw2[modes:, modes:]
    gram_im = raw2[:modes, modes:] - raw2[modes:, :modes]
    low = modes // 2
    emb_ref[0:modes, 0:modes] = gram_re
    emb_ref[0:modes, modes:order] = gram_im
    gram_in[0, :, 0:order] = emb_ref[0:low, 0:order]
    gram_in[0, :, order : 2 * order] = emb_ref[low:modes, 0:order]
    last = []
    for d in range(1, np_):
        copy = remote(
            gram_in.at[0], gram_in.at[d], gs.at[0, d], gs.at[1, d], "pix", peers[d - 1]
        )
        copy.start()
        last.append(copy)
    total = gram_in[0]
    for d in range(1, np_):
        last[d - 1].wait_recv()
        total = total + gram_in[d]
    emb_ref[0:low, 0:order] = total[:, 0:order]
    emb_ref[low:modes, 0:order] = total[:, order : 2 * order]
    gram_re = emb_ref[0:modes, 0:modes]
    gram_im = emb_ref[0:modes, modes:order]
    emb_ref[0:modes, modes:order] = gram_im
    emb_ref[modes:order, 0:modes] = -gram_im
    emb_ref[modes:order, modes:order] = gram_re
    first_root = turn_ref[...]
    first_t = first_root.T
    raw = 0.5 * jnp.dot(
        jnp.dot(first_t, emb_ref[...], precision=HIGH), first_root, precision=HIGH
    )
    gram_re = raw[:modes, :modes] + raw[modes:, modes:]
    gram_im = raw[:modes, modes:] - raw[modes:, :modes]
    emb_ref[0:modes, 0:modes] = gram_re
    emb_ref[0:modes, modes:order] = -gram_im
    emb_ref[modes:order, 0:modes] = gram_im
    emb_ref[modes:order, modes:order] = gram_re
    embedded = emb_ref[...]
    diagonal = row_id == col_id
    trace = jnp.sum(
        jnp.sum(jnp.where(diagonal, embedded, 0.0), axis=1, keepdims=True), axis=0, keepdims=True
    )
    identity = jnp.where(diagonal, 1.0, 0.0).astype(jnp.float32)
    second_root = newton_schulz(embedded / trace, identity) / jnp.sqrt(trace)
    turn_ref[...] = jnp.dot(second_root.T, first_t, precision=HIGH)
    for part_of in range(2):
        emb_ref[pl.ds(part_of * share, share), :] = turn_ref[
            pl.ds(part_of * modes + me * share, share), :
        ]
    mine = emb_ref[0 : 2 * share, :]
    upper = mine.astype(jnp.bfloat16)
    lower = (mine - upper.astype(jnp.float32)).astype(jnp.bfloat16)
    group = next(count for count in (8, 5, 4, 2, 1) if rows % count == 0)

    def rotate(step, carry):
        start = pl.multiple_of(step * (group * cols), 128)
        if chunk % 16 == 0:
            fields = jnp.concatenate(
                [applied_ref[j, :, pl.ds(start, group * cols)] for j in range(ne)], axis=0
            )
        else:
            fields = jnp.concatenate(
                [
                    applied_ref[j, :, pl.ds(start, group * cols)].astype(jnp.float32)
                    for j in range(ne)
                ],
                axis=0,
            ).astype(jnp.bfloat16)
        turned = dot(upper, fields, NN) + dot(lower, fields, NN)
        for i in range(group):
            for b in range(cols // 128):
                lines_ref[b, pl.ds((step * group + i) * 2 * share, 2 * share), :] = turned[
                    :, i * cols + b * 128 : i * cols + (b + 1) * 128
                ]
        return carry

    lax.fori_loop(0, rows // group, rotate, 0)
    chirp_re, chirp_im = chirp_ref[0], chirp_ref[1]
    for m in range(share):
        real = jnp.concatenate(
            [lines_ref[b, pl.ds(m, rows, stride=2 * share), :] for b in range(cols // 128)], axis=1
        )
        imag = jnp.concatenate(
            [
                lines_ref[b, pl.ds(share + m, rows, stride=2 * share), :]
                for b in range(cols // 128)
            ],
            axis=1,
        )
        launch_ref[m * rows : (m + 1) * rows, 0:cols] = chirp_re * real - chirp_im * imag
        launch_ref[m * rows : (m + 1) * rows, cols : 2 * cols] = chirp_re * imag + chirp_im * real
    launch = launch_ref[...]
    upper = launch.astype(jnp.bfloat16)
    lower = (launch - upper.astype(jnp.float32)).astype(jnp.bfloat16)
    spec_ref[...] = (
        dot(upper, table_ref[0], NN) + dot(upper, table_ref[1], NN) + dot(lower, table_ref[0], NN)
    )
    thin = cols // np_
    for p in range(np_):
        for c in range(2):
            for m in range(share):
                at = (2 * p + c) * thin
                to = (c * share + m) * thin
                send_ref[p, :, to : to + thin] = spec_ref[
                    m * rows : (m + 1) * rows, at : at + thin
                ].astype(jnp.bfloat16)
    swaps = []
    for d in range(1, np_):
        copy = remote(
            send_ref.at[peers[d - 1]], out_ref.at[me_p], gs.at[2, d], gs.at[3, d], "pix",
            peers[d - 1],
        )
        copy.start()
        swaps.append(copy)
    out_ref[me_p] = send_ref[me_p]
    for d in range(1, np_):
        source = lax.rem(me_p + np_ - d, np_)
        block = out_ref.at[source]
        remote(block, block, gs.at[2, d], gs.at[3, d], "pix", source).wait_recv()
    for copy in started + last + swaps:
        copy.wait_send()


def middle(waves, low, chirp, tables, mode_count):
    np_ = lax.axis_size("pix")
    ne = lax.axis_size("elec")
    electrons = waves.shape[0]
    pixels = waves.shape[1] // 2
    order = 2 * mode_count
    chunk = order // ne
    depth = order // np_
    pieces = next(count for count in (4, 2, 1) if pixels % (128 * count) == 0)
    sub = next(size for size in (1280, 640, 512, 256, 128) if pixels // pieces % size == 0)
    chips = ne // 2
    wide = electrons + order + -order % 128
    share = mode_count // ne
    rows, cols = chirp.shape[1:]
    lanes = 2 * share * (cols // np_)
    vmem = pl.BlockSpec(memory_space=pltpu.VMEM)
    dma = pltpu.SemaphoreType.DMA
    f32, bf16 = jnp.float32, jnp.bfloat16
    return pl.pallas_call(
        functools.partial(core_kernel, np_, ne, pieces, sub, electrons, mode_count),
        out_shape=jax.ShapeDtypeStruct((np_, rows, lanes), bf16),
        in_specs=[vmem] * 4,
        out_specs=vmem,
        scratch_shapes=[
            pltpu.VMEM((ne, chunk, pixels), bf16),
            pltpu.VMEM((order, order), f32),
            pltpu.VMEM((np_, depth, electrons), f32),
            pltpu.VMEM((cols // 128, rows * 2 * share, 128), f32),
            pltpu.VMEM((share * rows, 2 * cols), f32),
            pltpu.VMEM((share * rows, 2 * cols), f32),
            pltpu.VMEM((np_, rows, lanes), bf16),
            pltpu.VMEM((order, wide), f32),
            pltpu.VMEM((2 * order, electrons), bf16),
            pltpu.VMEM((order, sub), f32),
            pltpu.VMEM((order, order), f32),
            pltpu.VMEM((np_, depth, electrons), f32),
            pltpu.VMEM((np_, depth, electrons), f32),
            pltpu.VMEM((np_, depth, wide), f32),
            pltpu.VMEM((np_, depth, wide), f32),
            pltpu.VMEM((np_, depth, wide), f32),
            pltpu.VMEM((2, ne, chunk, pixels), bf16),
            pltpu.VMEM((2, chips, chunk, pixels), bf16),
            pltpu.VMEM((2, chips, chunk, pixels), bf16),
            pltpu.VMEM((2, chips, chunk, pixels), bf16),
            pltpu.VMEM((ne, chunk, pixels), bf16),
            pltpu.VMEM((np_, mode_count // 2, 2 * order), f32),
            dma((8, np_)),
            dma((20, chips * pieces)),
            dma((4, np_)),
        ],
        compiler_params=pltpu.CompilerParams(
            collective_id=1, has_side_effects=True, vmem_limit_bytes=60 * 1024 * 1024
        ),
        name="middle",
    )(waves, low, chirp, tables)


def newton_schulz(scaled, identity):
    inverse_root = identity
    for step in range(NS_STEPS):
        product = scaled if step == 0 else jnp.dot(inverse_root, scaled, precision=HIGH)
        correction = 1.5 * identity - 0.5 * product
        if step == 0:
            inverse_root = correction
        else:
            inverse_root = jnp.dot(correction, inverse_root, precision=HIGH)
        if step + 1 < NS_STEPS:
            scaled = jnp.dot(scaled, correction, precision=HIGH)
    return inverse_root


def dft_table(length):
    index = np.arange(length, dtype=np.int64)
    angle = 2.0 * np.pi / length * (index[:, None] * index[None, :] % length)
    return np.cos(angle).astype(np.float32), -np.sin(angle).astype(np.float32)


def split(table):
    upper = table.astype(jnp.bfloat16)
    lower = (table - upper.astype(np.float32)).astype(jnp.bfloat16)
    return upper, lower


def chirp_phase(row_pos, col_pos, row_total, col_total, factor):
    row_term = (row_pos - row_total / 2.0) ** 2 / row_total
    col_term = (col_pos - col_total / 2.0) ** 2 / col_total
    angle = math.pi * factor * (row_term[:, None] + col_term[None, :])
    return (jnp.cos(angle), jnp.sin(angle))


def column_tables(length, pix_count):
    table_re, table_im = dft_table(length)
    full = np.stack([np.stack([table_re, table_im], 1), np.stack([-table_im, table_re], 1)])
    full = full.reshape(2, length, 2, pix_count, length // pix_count).transpose(0, 1, 3, 2, 4)
    return np.stack(split(full.reshape(2 * length, 2 * length)))


def row_section(spectrum, share, col_pos, row_total, col_total):
    width = col_pos.shape[0]
    table_re, table_im = dft_table(row_total)
    upper, lower = split(np.concatenate([table_re, table_im], axis=0))
    tables = np.concatenate([upper, lower], axis=0)
    wide = jnp.dot(jnp.asarray(tables), spectrum, preferred_element_type=jnp.float32)
    wide = wide[: 2 * row_total] + wide[2 * row_total :]
    half = share * width
    out_re = wide[:row_total, :half] - wide[row_total:, half:]
    out_im = wide[:row_total, half:] + wide[row_total:, :half]
    row_pos = jnp.arange(row_total, dtype=jnp.float32)
    chirp_re, chirp_im = chirp_phase(row_pos, col_pos, row_total, col_total, 0.25)
    out_re = out_re.reshape(row_total, share, width).transpose(1, 0, 2)
    out_im = out_im.reshape(row_total, share, width).transpose(1, 0, 2)
    return jnp.stack([chirp_re * out_re - chirp_im * out_im, chirp_re * out_im + chirp_im * out_re])


def shards(wavefronts, trial_modes):
    electrons_dev, _, rows_dev, cols = wavefronts.shape
    mode_count = trial_modes.shape[1]
    order = 2 * mode_count
    pixels = rows_dev * cols
    groups = lax.axis_size("elec")
    share = mode_count // groups
    waves = wavefronts.reshape(electrons_dev, 2 * pixels)
    low = trial_modes.astype(jnp.bfloat16).reshape(order, pixels)

    pix_count = lax.axis_size("pix")
    row_total = rows_dev * pix_count
    row_pos = (lax.axis_index("pix") * rows_dev + jnp.arange(rows_dev, dtype=jnp.int32)).astype(
        jnp.float32
    )
    chirp = jnp.stack(
        chirp_phase(row_pos, jnp.arange(cols, dtype=jnp.float32), row_total, cols, 0.5)
    )
    tables = jnp.asarray(column_tables(cols, pix_count))
    column_block = middle(waves, low, chirp, tables, mode_count).reshape(row_total, -1)
    width = cols // pix_count
    col_pos = (lax.axis_index("pix") * width + jnp.arange(width, dtype=jnp.int32)).astype(
        jnp.float32
    )
    return row_section(column_block, share, col_pos, row_total, cols)


def solution(mesh):
    in_specs = (P("elec", None, "pix", None), P(None, None, "pix", None))
    out_specs = P(None, "elec", None, "pix")
    return jax.shard_map(shards, mesh=mesh, in_specs=in_specs, out_specs=out_specs, check_vma=False)
```
